32 devices in a mesh: tm: 8 (over z, core), row: 4 (over y, x).
Axes of the slice: x: 2, y: 2, z: 4, core: 2. Of those that a mesh axis runs over, the one named last changes fastest.
Arguments:
- prior_ensemble: float32 [64, 128, 4096], P('tm', None, 'row'), may hold values from -6 to 6
- observation_data: float32 [64, 8192], P('tm', 'row'), may hold values from -24 to 24
- inverse_error_spread: float32 [8192], P('row'), may hold values from 0.024902152 to 0.24902152
- anomaly_inflation: float32 [64], P('tm'), may hold values from 1.1 to 1.4
- nonzero_tiles: float32 [64, 8, 128, 128], P('row'), may hold values from -0.1875 to 0.1875
- nonzero_tile_targets: int32 [64, 8], P('row'), may hold values from 0 to 31, as said below
Outputs:
- smoothed_ensemble: float32 [64, 128, 4096], P('tm', None, 'row')
- filtered_ensemble: float32 [64, 128, 4096], P('tm', None, 'row')
The draws below stay inside these ranges and needn't reach their ends.
Inputs may be any that keep to these rules, and one draw needn't show every extreme that they name: `nonzero_tile_targets`: in each block row the 8 block columns are distinct.
All inputs are finite; a program needn't handle non-finite values. Where the reference program divides by a largest or mean magnitude, that divisor is 1e-20 or more.
Results may differ from the reference program's by a relative error of at most 0.0003.
Values sent between devices are 32-bit elements; how exact they have to be, the bound alone decides.
No kernel may reach another device: no remote copies, remote signals or barrier semaphores. Data moves between devices by JAX's collectives and lax.ppermute only.
A program may use at most 128 MiB of HBM per device.

```python
import math
import jax
import jax.numpy as jnp
from jax import lax

DIMENSION = 4096
NOBS = 8192
BLK = 128
NNZB = 8
ENSEMBLE_SIZE = 128
NS_ITERS = 8
HORIZON_LENGTH = 64
NBR = 64
NBC = 32


def draw_nonzero_tile_targets(key, part):
    row_keys = jax.random.split(key, NBR)
    picked = jax.vmap(lambda row_key: jax.random.permutation(row_key, NBC)[:NNZB])(row_keys)
    return picked.astype(jnp.int32)


def levels(key, dims, shards, least, high):
    gain, own = 1.0, jax.random.fold_in(key, 6)
    for dim, blocks in shards:
        steps = jnp.exp(jax.random.uniform(jax.random.fold_in(own, dim), (blocks,), jnp.float32, least / len(shards), high / len(shards)))
        gain = gain * jnp.repeat(steps, dims[dim] // blocks).reshape([-1 if axis == dim else 1 for axis in range(len(dims))])
    return gain


def noise(own_key, extent, width, bound, cuts=(), kind=jnp.bfloat16):
    array = jax.random.normal(own_key, extent, jnp.float32) * width
    if len(cuts) > 0:
        array = levels(own_key, extent, cuts, -0.22, 0.18) * array
    return jnp.clip(array, min=-bound, max=bound).astype(kind)


def setup_inputs(seed: int = 0) -> dict:
    splits = jax.random.split(jax.random.key(seed), 7)
    prior_ensemble = noise(splits[0], (HORIZON_LENGTH, ENSEMBLE_SIZE, DIMENSION), 1.0, 6.0, ((0, 8), (2, 4)), jnp.float32)
    observation_data = noise(splits[1], (HORIZON_LENGTH, NOBS), 4.0, 24.0, ((0, 8), (1, 4)), jnp.float32)
    inverse_error_spread = jnp.clip(jnp.exp(math.log(0.24902152) - 2.3025851 * jax.random.uniform(splits[2], (NOBS,), jnp.float32) ** levels(splits[2], (NOBS,), ((0, 4),), -0.2, 0.2)), 0.024902152, 0.24902152)
    anomaly_inflation = jnp.clip(1.1 + 0.29999995 * jax.random.uniform(splits[3], (HORIZON_LENGTH,), jnp.float32) ** levels(splits[3], (HORIZON_LENGTH,), ((0, 8),), -0.2, 0.2), 1.1, 1.4)
    nonzero_tiles = noise(splits[4], (NBR, NNZB, BLK, BLK), (NNZB * BLK) ** -0.5, 0.1875, ((0, 4),), jnp.float32)
    nonzero_tile_targets = draw_nonzero_tile_targets(jax.random.fold_in(splits[6], 71), 0)
    return dict(prior_ensemble=prior_ensemble, observation_data=observation_data, inverse_error_spread=inverse_error_spread, anomaly_inflation=anomaly_inflation, nonzero_tiles=nonzero_tiles, nonzero_tile_targets=nonzero_tile_targets)


exact_product = lax.Precision.HIGHEST

def ensemble_transforms(info_matrix, info_vector, anomaly_inflation):
    ensemble_entries = info_matrix.shape[-1]
    identity = jnp.eye(ensemble_entries, dtype=jnp.float32)
    row_bound = lax.optimization_barrier(jnp.max(lax.optimization_barrier(jnp.sum(jnp.abs(info_matrix), axis=2)), axis=1))
    scaled = info_matrix / row_bound[:, None, None]
    root_iter = scaled
    inv_iter = jnp.broadcast_to(identity, scaled.shape)
    for _ in range(NS_ITERS):
        update = 1.5 * identity - 0.5 * jnp.matmul(inv_iter, root_iter, precision=exact_product)
        root_iter = jnp.matmul(root_iter, update, precision=exact_product)
        inv_iter = jnp.matmul(update, inv_iter, precision=exact_product)
    inverse_root = inv_iter / jnp.sqrt(row_bound)[:, None, None]
    half_weights = jnp.einsum('tab,tb->ta', inverse_root, info_vector, precision=exact_product)
    mean_weights = jnp.einsum('tab,tb->ta', inverse_root, half_weights, precision=exact_product)
    spread_norm = float(ensemble_entries - 1) ** 0.5
    mixing = mean_weights[:, :, None] / spread_norm + anomaly_inflation[:, None, None] * inverse_root
    mixing = mixing - lax.optimization_barrier(jnp.mean(mixing, axis=1, keepdims=True))
    return mixing + 1.0 / ensemble_entries

def observe_ensemble(ensemble_vectors, nonzero_tiles, nonzero_tile_targets):
    ensemble_entries = ensemble_vectors.shape[0]
    blocks = ensemble_vectors.reshape(ensemble_entries, NBC, BLK)[:, nonzero_tile_targets]
    result = jnp.einsum('mbkj,bkij->mbi', blocks, nonzero_tiles, precision=exact_product)
    return result.reshape(ensemble_entries, NOBS)

def reference(prior_ensemble, observation_data, inverse_error_spread, anomaly_inflation, nonzero_tiles, nonzero_tile_targets):
    predicted_observations = lax.map(lambda ensemble_vectors: observe_ensemble(ensemble_vectors, nonzero_tiles, nonzero_tile_targets), prior_ensemble)
    obs_mean = lax.optimization_barrier(jnp.mean(predicted_observations, axis=1))
    whitened = (predicted_observations - obs_mean[:, None, :]) * inverse_error_spread / float(ENSEMBLE_SIZE - 1) ** 0.5
    innovation = (observation_data - obs_mean) * inverse_error_spread
    info_matrix = jnp.einsum('tmo,tno->tmn', whitened, whitened, precision=exact_product)
    info_matrix = info_matrix + jnp.eye(ENSEMBLE_SIZE, dtype=jnp.float32)
    info_vector = jnp.einsum('tmo,to->tm', whitened, innovation, precision=exact_product)
    ensemble_weight_factors = ensemble_transforms(info_matrix, info_vector, anomaly_inflation)
    filtered_ensemble = jnp.einsum('fjn,fjt->fnt', ensemble_weight_factors, prior_ensemble, precision=exact_product)

    def backward(running, transform):
        product = jnp.matmul(transform, running, precision=exact_product)
        return (product, product)
    _, suffix_product = lax.scan(backward, jnp.eye(ENSEMBLE_SIZE, dtype=jnp.float32), ensemble_weight_factors, reverse=True)
    smoothed_ensemble = jnp.einsum('fjn,fjt->fnt', suffix_product, prior_ensemble, precision=exact_product)
    return (smoothed_ensemble, filtered_ensemble)
```

```python
import functools

import jax
import jax.numpy as jnp
from jax import lax
from jax.experimental import pallas as pl
from jax.experimental.pallas import tpu as pltpu
from jax.sharding import PartitionSpec as P


NS_ITERS = 8
F32, BF16 = jnp.float32, jnp.bfloat16
exact_product = lax.Precision.HIGHEST
MEAN_ROWS = 16
VMEM_LIMIT = 48 << 20


def split(value):
    high = value.astype(BF16)
    return high, (value - high.astype(F32)).astype(BF16)


def product(left, right):
    return jnp.dot(left, right, precision=exact_product, preferred_element_type=F32)


def by_rows(left, right):
    return lax.dot_general(left, right, (((1,), (1,)), ((), ())), preferred_element_type=F32)


def eye(size):
    rows = lax.broadcasted_iota(jnp.int32, (size, size), 0)
    columns = lax.broadcasted_iota(jnp.int32, (size, size), 1)
    return (rows == columns).astype(F32)


def params(**more):
    return pltpu.CompilerParams(vmem_limit_bytes=VMEM_LIMIT, **more)


def prepare_body(count, each, order_ref, spread_ref, *refs):
    tiles, out = refs[:count], refs[-1]
    step = pl.program_id(0)
    size = spread_ref.shape[-1]
    scale = jnp.transpose(jnp.broadcast_to(spread_ref[0], (size, size)))

    def emit(tile_ref):
        for k in range(tile_ref.shape[1]):
            high, low = split(tile_ref[0, k] * scale)
            out[0, :size, k * size : (k + 1) * size] = high
            out[0, size:, k * size : (k + 1) * size] = low

    for number, tile_ref in enumerate(tiles):
        pl.when(step // each == number)(functools.partial(emit, tile_ref))


def prepare(pieces, order, spread, half, halves, base, into):
    count, (each, k, size, _) = len(pieces), pieces[0].shape
    width = k * size

    def row(step, order_ref):
        return base + order_ref[step // each] * each + step % each

    in_specs = [pl.BlockSpec((1, 1, size), lambda s, o: (row(s, o), 0, 0))]
    for number in range(count):
        in_specs.append(
            pl.BlockSpec(
                (1, k, size, size),
                lambda s, o, number=number: (jnp.clip(s - number * each, 0, each - 1), 0, 0, 0),
            )
        )
    args = [order, spread, *pieces]
    aliases = {}
    total = spread.shape[0]
    if into is not None:
        in_specs.append(pl.BlockSpec(memory_space=pl.ANY))
        args.append(into)
        aliases = {len(args) - 1: 0}
    return pl.pallas_call(
        functools.partial(prepare_body, count, each),
        grid_spec=pltpu.PrefetchScalarGridSpec(
            num_scalar_prefetch=1,
            grid=(count * each,),
            in_specs=in_specs,
            out_specs=pl.BlockSpec((1, 2 * size, width), lambda s, o: (row(s, o), 0, half)),
        ),
        out_shape=jax.ShapeDtypeStruct((total, 2 * size, halves * width), BF16),
        input_output_aliases=aliases,
        compiler_params=params(),
        cost_estimate=pl.CostEstimate(
            flops=0, transcendentals=0, bytes_accessed=count * each * k * size * size * 8
        ),
        name="prepare",
    )(*args)


def observe_body(steps, shards, pairs, target_ref, row_ref, tiles_ref, data_ref, *refs):
    states = refs[: steps * shards]
    out, high_ref, low_ref, gram_ref = refs[steps * shards :]
    size = out.shape[-1]
    members = size
    rows = steps * members
    blocks = states[0].shape[-1] // size
    step = pl.program_id(0)
    slot_row = lax.broadcasted_iota(jnp.int32, (MEAN_ROWS, size), 0)

    @pl.when(step == 0)
    def _():
        for mask in range(shards):
            first = (row_ref[0] ^ mask) * blocks
            for block in range(blocks):
                columns = slice(block * size, (block + 1) * size)
                means = jnp.zeros((MEAN_ROWS, size), F32)
                for i in range(steps):
                    state = states[i * shards + mask]
                    value = state[0, :, columns] if len(state.shape) == 3 else state[:, columns]
                    mean = jnp.mean(value, axis=0, keepdims=True)
                    high, low = split(value - mean)
                    high_ref[first + block, i * members : (i + 1) * members] = high
                    low_ref[first + block, i * members : (i + 1) * members] = low
                    means = jnp.where(slot_row == i, mean, means)
                high, low = split(means)
                high_ref[first + block, rows:] = high
                low_ref[first + block, rows:] = low
        gram_ref[...] = jnp.zeros_like(gram_ref)

    nonzero = target_ref.shape[1]
    seen = []
    for j in range(pairs):
        at = step * pairs + j
        slots = [target_ref[at, k] for k in range(nonzero)]
        high = jnp.concatenate([high_ref[slot] for slot in slots], axis=1)
        low = jnp.concatenate([low_ref[slot] for slot in slots], axis=1)
        first = by_rows(high, tiles_ref[j])
        second = by_rows(low, tiles_ref[j, :size])
        seen.append(first[:, :size] + first[:, size:] + second)
    for i in range(steps):
        white = [value[i * members : (i + 1) * members] for value in seen]
        white_high, white_low = split(jnp.concatenate(white, axis=1))
        innovation = [
            data_ref[i, j] - seen[j][rows + i : rows + i + 1] for j in range(pairs)
        ]
        inn_high, inn_low = split(jnp.concatenate(innovation, axis=1))
        wide_row = lax.broadcasted_iota(jnp.int32, (MEAN_ROWS, pairs * size), 0)
        extra = jnp.where(
            wide_row == 0,
            inn_high.astype(F32),
            jnp.where(wide_row == 1, inn_low.astype(F32), 0.0),
        ).astype(BF16)
        left = jnp.concatenate([white_high, extra], axis=0)
        right = jnp.concatenate([white_high, white_low], axis=0)
        gram_ref[i] += by_rows(left, right)

    @pl.when(step == pl.num_programs(0) - 1)
    def _():
        for i in range(steps):
            total = gram_ref[i]
            cross = total[:members, members:]
            out[i, :members] = total[:members, :members] + cross + jnp.transpose(cross)
            vector = (
                total[members : members + 1, :members]
                + total[members : members + 1, members:]
                + total[members + 1 : members + 2, :members]
            )
            out[i, members:] = jnp.broadcast_to(vector, (8, members))


def observe(chunk, states, tiles, targets, data, row):
    steps, shards = len(chunk), len(states[0])
    total, double, width = tiles.shape
    size = double // 2
    pairs = 2
    members = size
    columns = states[0][1].shape[-1]
    in_specs = [
        pl.BlockSpec((pairs, double, width), lambda s, *_: (s, 0, 0)),
        pl.BlockSpec((steps, pairs, 1, size), lambda s, *_: (0, s, 0, 0)),
    ]
    flat = []
    for g, pieces in zip(chunk, states):
        for piece in pieces:
            flat.append(piece)
            if piece.ndim == 3:
                in_specs.append(
                    pl.BlockSpec((1, members, columns), lambda s, *_, g=g: (g, 0, 0), pipeline_mode=pl.Buffered(1))
                )
            else:
                in_specs.append(
                    pl.BlockSpec((members, columns), lambda s, *_: (0, 0), pipeline_mode=pl.Buffered(1))
                )
    slots = shards * (columns // size)
    rows = steps * members + MEAN_ROWS
    flops = 2 * 3 * rows * size * width * total
    return pl.pallas_call(
        functools.partial(observe_body, steps, shards, pairs),
        grid_spec=pltpu.PrefetchScalarGridSpec(
            num_scalar_prefetch=2,
            grid=(total // pairs,),
            in_specs=in_specs,
            out_specs=pl.BlockSpec((steps, members + 8, members), lambda s, *_: (0, 0, 0)),
            scratch_shapes=[
                pltpu.VMEM((slots, rows, size), BF16),
                pltpu.VMEM((slots, rows, size), BF16),
                pltpu.VMEM((steps, members + MEAN_ROWS, 2 * members), F32),
            ],
        ),
        out_shape=jax.ShapeDtypeStruct((steps, members + 8, members), F32),
        compiler_params=params(),
        cost_estimate=pl.CostEstimate(
            flops=flops, transcendentals=0, bytes_accessed=total * double * width * 2
        ),
        name="observe",
    )(targets, row, tiles, data, *flat)


def transform_body(steps, parts, inflation_ref, *refs):
    ins, out = refs[:parts], refs[parts]
    size = out.shape[-1]
    identity = eye(size)
    spans = range(steps)
    sums = [sum((ref[i] for ref in ins[1:]), ins[0][i]) for i in spans]
    info = [value[:size] + identity for value in sums]
    vector = [value[size:] for value in sums]
    bound = [
        jnp.max(jnp.sum(jnp.abs(value), axis=1, keepdims=True), axis=0, keepdims=True)
        for value in info
    ]
    scaled = [value / top for value, top in zip(info, bound)]
    update = [1.5 * identity - 0.5 * value for value in scaled]
    inverse = update
    root = [product(value, up) for value, up in zip(scaled, update)]
    for number in range(1, NS_ITERS):
        update = [1.5 * identity - 0.5 * product(q, y) for q, y in zip(inverse, root)]
        if number < NS_ITERS - 1:
            root = [product(y, up) for y, up in zip(root, update)]
        inverse = [product(up, q) for q, up in zip(inverse, update)]
    for i in spans:
        half_root = inverse[i] / jnp.sqrt(bound[i])
        half = lax.dot_general(
            vector[i], half_root, (((1,), (1,)), ((), ())), precision=exact_product,
            preferred_element_type=F32,
        )
        weights = jnp.sum(half_root * half[:1], axis=1, keepdims=True)
        mixing = weights + inflation_ref[i] * half_root
        mixing = mixing - jnp.mean(mixing, axis=0, keepdims=True)
        out[i] = mixing + 1.0 / size


def transforms(parts, inflation):
    steps, _, members = parts[0].shape
    vmem = pl.BlockSpec(memory_space=pltpu.VMEM)
    return pl.pallas_call(
        functools.partial(transform_body, steps, len(parts)),
        in_specs=[pl.BlockSpec(memory_space=pltpu.SMEM)] + [vmem] * len(parts),
        out_specs=vmem,
        out_shape=jax.ShapeDtypeStruct((steps, members, members), F32),
        compiler_params=params(),
        cost_estimate=pl.CostEstimate(
            flops=steps * 21 * 6 * 2 * members**3 * 4, transcendentals=0,
            bytes_accessed=steps * members * members * 12,
        ),
        name="transforms",
    )(inflation, *parts)


def chain_body(steps, first, low_ref, *refs):
    mine, other = refs[:2]
    out = refs[-1]
    running = None if first else refs[2][0]
    even = low_ref[0] == 0
    for i in reversed(range(steps)):
        earlier = jnp.where(even, mine[i], other[i])
        later = jnp.where(even, other[i], mine[i])
        after = later if running is None else product(later, running)
        out[2 * i + 1] = after
        running = product(earlier, after)
        out[2 * i] = running


def chain(mine, other, running, low):
    steps, size, _ = mine.shape
    vmem = pl.BlockSpec(memory_space=pltpu.VMEM)
    args = [mine, other] + ([] if running is None else [running])
    return pl.pallas_call(
        functools.partial(chain_body, steps, running is None),
        in_specs=[pl.BlockSpec(memory_space=pltpu.SMEM)] + [vmem] * len(args),
        out_specs=vmem,
        out_shape=jax.ShapeDtypeStruct((2 * steps, size, size), F32),
        compiler_params=params(),
        cost_estimate=pl.CostEstimate(
            flops=steps * 2 * 6 * 2 * size**3 * 8, transcendentals=0,
            bytes_accessed=steps * size * size * 16,
        ),
        name="chain",
    )(low, *args)


def couple_body(core_ref, mine, other, out):
    first = core_ref[0] == 0
    out[...] = product(
        jnp.where(first, mine[...], other[...]), jnp.where(first, other[...], mine[...])
    )


def couple(mine, other, core):
    vmem = pl.BlockSpec(memory_space=pltpu.VMEM)
    return pl.pallas_call(
        couple_body,
        in_specs=[pl.BlockSpec(memory_space=pltpu.SMEM), vmem, vmem],
        out_specs=vmem,
        out_shape=jax.ShapeDtypeStruct(mine.shape, F32),
        compiler_params=params(),
        name="couple",
    )(core, mine, other)


def weigh(weights, state_ref, out_ref):
    high, low = split(jnp.transpose(weights))
    state_high, state_low = split(state_ref[0])
    out_ref[0] = jnp.dot(
        jnp.concatenate([high, high], axis=1),
        jnp.concatenate([state_high, state_low], axis=0),
        preferred_element_type=F32,
    ) + jnp.dot(low, state_high, preferred_element_type=F32)


def filter_body(later_chunks, low_ref, *refs):
    state_ref, out_ref = refs[-2:]
    weigh(jnp.where(low_ref[0] == 0, refs[0][0], refs[1][0]), state_ref, out_ref)


def filtered(even, odd, prior):
    steps, members, columns = prior.shape
    weights = jnp.stack([even, odd], axis=1).reshape(steps, members, members)

    def body(weights_ref, state_ref, out_ref):
        weigh(weights_ref[0], state_ref, out_ref)

    return pl.pallas_call(
        body,
        grid=(steps,),
        in_specs=[
            pl.BlockSpec((1, members, members), lambda t: (t, 0, 0)),
            pl.BlockSpec((1, members, columns), lambda t: (t, 0, 0)),
        ],
        out_specs=pl.BlockSpec((1, members, columns), lambda t: (t, 0, 0)),
        out_shape=jax.ShapeDtypeStruct(prior.shape, F32),
        compiler_params=params(),
        cost_estimate=pl.CostEstimate(
            flops=steps * 3 * 2 * members * members * columns, transcendentals=0,
            bytes_accessed=prior.size * 8,
        ),
        name="filtered",
    )(weights, prior)


def smooth_body(groups, place_ref, suffix_ref, state_ref, partner_ref, *refs):
    later, out_ref, end_ref = refs[: groups - 1], refs[-2], refs[-1]
    size = suffix_ref.shape[-1]

    @pl.when(pl.program_id(0) == 0)
    def _():
        identity = eye(size)
        chain = [jnp.where(place_ref[1] == 0, partner_ref[...], identity)]
        for ahead, ref in enumerate(later, 1):
            chain.append(jnp.where(place_ref[0] + ahead < groups, ref[...], identity))
        while len(chain) > 1:
            joined = [product(a, b) for a, b in zip(chain[::2], chain[1::2])]
            chain = joined + ([chain[-1]] if len(chain) % 2 else [])
        end_ref[...] = chain[0]

    weigh(product(suffix_ref[0], end_ref[...]), state_ref, out_ref)


def smoothed(suffix, prior, partner, later, place):
    steps, members, columns = prior.shape
    groups = len(later) + 1
    vmem = pl.BlockSpec((members, members), lambda t: (0, 0))
    return pl.pallas_call(
        functools.partial(smooth_body, groups),
        grid=(steps,),
        in_specs=[
            pl.BlockSpec(memory_space=pltpu.SMEM),
            pl.BlockSpec((1, members, members), lambda t: (t, 0, 0)),
            pl.BlockSpec((1, members, columns), lambda t: (t, 0, 0)),
        ]
        + [vmem] * groups,
        out_specs=pl.BlockSpec((1, members, columns), lambda t: (t, 0, 0)),
        out_shape=jax.ShapeDtypeStruct(prior.shape, F32),
        scratch_shapes=[pltpu.VMEM((members, members), F32)],
        compiler_params=params(),
        cost_estimate=pl.CostEstimate(
            flops=steps * 3 * 2 * members * members * columns, transcendentals=0,
            bytes_accessed=prior.size * 8,
        ),
        name="smoothed",
    )(place, suffix, prior, partner, *later)


def exchange(value, axis, bit):
    count = lax.axis_size(axis)
    return lax.ppermute(value, axis, [(i, i ^ bit) for i in range(count)])


def local(
    prior_ensemble,
    observation_data,
    inverse_error_spread,
    anomaly_inflation,
    nonzero_tiles,
    nonzero_tile_targets,
):
    steps, members, columns = prior_ensemble.shape
    block_rows, nonzero, size, _ = nonzero_tiles.shape
    shards = lax.axis_size("row")
    row, place = lax.axis_index("row"), lax.axis_index("tm")
    low, core = row & 1, place & 1
    pairs = steps // 2
    chunks = ((3, 2), (1,), (0,))

    spread = inverse_error_spread / float(members - 1) ** 0.5
    data = observation_data * spread
    halves = data.reshape(pairs, 2, -1)
    of_low = functools.partial(lax.dynamic_index_in_dim, axis=1, keepdims=False)
    padded = jnp.zeros((data.shape[1],), F32)
    padded = padded.at[: nonzero_tile_targets.size].set(nonzero_tile_targets.reshape(-1).astype(F32))
    note = jnp.concatenate([of_low(halves, 1 - low), spread[None], padded[None]], axis=0)
    quarter = place & 3
    each = block_rows // 4
    group = lax.dynamic_slice_in_dim(nonzero_tiles, quarter * each, each, axis=0)
    middle = nonzero // 2
    note = exchange(note, "row", 1)
    fetched = [exchange(group[:, :middle], "row", 1), exchange(group[:, middle:], "row", 1)]
    states = prior_ensemble.reshape(pairs, 2, members, columns)
    mine, theirs = of_low(states, low), of_low(states, 1 - low)
    pieces = {}
    own_moved = {}
    bit = 2
    while bit < shards:
        own_moved[bit] = exchange(mine, "row", bit)
        bit *= 2
    sent = {}
    for chunk in chunks:
        for g in chunk:
            sent[g] = exchange(theirs[g], "row", 1)
    for chunk in chunks:
        for g in chunk:
            have = [mine, sent[g]]
            bit = 2
            while bit < shards:
                moved = [own_moved[bit]]
                for value in have[1:]:
                    if value.ndim == 3:
                        value = value[g]
                    moved.append(exchange(value, "row", bit))
                have = have + moved
                bit *= 2
            pieces[g] = have

    note_data = note[:pairs].reshape(pairs, block_rows, 1, size)
    own_data = of_low(halves, low).reshape(pairs, block_rows, 1, size)
    all_data = jnp.concatenate([own_data, note_data], axis=1)
    all_spread = jnp.concatenate([spread, note[pairs]]).reshape(2 * block_rows, 1, size)
    their_targets = note[pairs + 1, : nonzero_tile_targets.size].astype(jnp.int32)
    targets = jnp.concatenate(
        [nonzero_tile_targets, their_targets.reshape(block_rows, nonzero)], axis=0
    )
    tiles = prepare(
        [nonzero_tiles], jnp.zeros((1,), jnp.int32), all_spread, 0, 1, 0, None
    )
    order = jnp.stack([quarter, quarter ^ 2, quarter ^ 1, quarter ^ 3]).astype(jnp.int32)
    for half, value in enumerate(fetched):
        across = exchange(value, "tm", 2)
        parts = [value, across, exchange(value, "tm", 1), exchange(across, "tm", 1)]
        tiles = prepare(parts, order, all_spread, half, 2, block_rows, tiles)

    row_scalar = row.astype(jnp.int32).reshape(1)
    low_scalar = low.astype(jnp.int32).reshape(1)
    inflation = of_low(anomaly_inflation.reshape(pairs, 2), low)
    running, suffix = None, [None] * pairs
    own_steps, their_steps = [None] * pairs, [None] * pairs
    for chunk in chunks:
        first, count = min(chunk), len(chunk)
        ordered = tuple(sorted(chunk))
        part = observe(
            ordered,
            [pieces[g] for g in ordered],
            tiles,
            targets,
            all_data[first : first + count],
            row_scalar,
        )
        bit = 2
        parts = [part]
        while bit < shards:
            moved = exchange(part, "row", bit)
            if bit * 2 < shards:
                part = part + moved
                parts = [part]
            else:
                parts = [part, moved]
            bit *= 2
        matrix = transforms(parts, inflation[first : first + count])
        other = exchange(matrix, "row", 1)
        products = chain(matrix, other, running, low_scalar)
        running = products[:1]
        for number, g in enumerate(ordered):
            suffix[g] = products[2 * number : 2 * number + 2]
            own_steps[g], their_steps[g] = matrix[number], other[number]

    whole = running[0]
    core_scalar = core.astype(jnp.int32).reshape(1)
    partner = exchange(whole, "tm", 1)
    coupled = couple(whole, partner, core_scalar)
    groups = lax.axis_size("tm") // 2
    later = []
    for ahead in range(1, groups):
        hop = 2 * ahead
        later.append(lax.ppermute(coupled, "tm", [(i + hop, i) for i in range(2 * groups - hop)]))
    own_steps, their_steps = jnp.stack(own_steps), jnp.stack(their_steps)
    even = jnp.where(low == 0, own_steps, their_steps)
    odd = jnp.where(low == 0, their_steps, own_steps)
    filtered_ensemble = filtered(even, odd, prior_ensemble)
    where = jnp.stack([place // 2, core]).astype(jnp.int32)
    smoothed_ensemble = smoothed(
        jnp.concatenate(suffix), prior_ensemble, partner, later, where
    )
    return (smoothed_ensemble, filtered_ensemble)


def solution(mesh):
    placed = (
        P("tm", None, "row"),
        P("tm", "row"),
        P("row"),
        P("tm"),
        P("row", None, None, None),
        P("row", None),
    )
    return jax.shard_map(
        local,
        mesh=mesh,
        in_specs=placed,
        out_specs=(P("tm", None, "row"), P("tm", None, "row")),
        check_vma=False,
    )
```

```python
import functools

import jax
import jax.numpy as jnp
from jax import lax
from jax.experimental import pallas as pl
from jax.experimental.pallas import tpu as pltpu
from jax.sharding import PartitionSpec as P


NS_ITERS = 8
F32, BF16 = jnp.float32, jnp.bfloat16
exact_product = lax.Precision.HIGHEST
MEAN_ROWS = 16
VMEM_LIMIT = 30 << 20


def split(value):
    high = value.astype(BF16)
    return high, (value - high.astype(F32)).astype(BF16)


def product(left, right):
    return jnp.dot(left, right, precision=exact_product, preferred_element_type=F32)


def by_rows(left, right):
    return lax.dot_general(left, right, (((1,), (1,)), ((), ())), preferred_element_type=F32)


def eye(size):
    rows = lax.broadcasted_iota(jnp.int32, (size, size), 0)
    columns = lax.broadcasted_iota(jnp.int32, (size, size), 1)
    return (rows == columns).astype(F32)


def params(**more):
    return pltpu.CompilerParams(vmem_limit_bytes=VMEM_LIMIT, **more)


def prepare_body(count, each, order_ref, spread_ref, *refs):
    tiles, out = refs[:count], refs[-1]
    step = pl.program_id(0)
    size = spread_ref.shape[-1]
    scale = jnp.transpose(jnp.broadcast_to(spread_ref[0], (size, size)))
    at = order_ref[step // each] * each + step % each

    def emit(tile_ref):
        for k in range(tile_ref.shape[1]):
            high, low = split(tile_ref[0, k] * scale)
            out[at, :size, k * size : (k + 1) * size] = high
            out[at, size:, k * size : (k + 1) * size] = low

    for number, tile_ref in enumerate(tiles):
        pl.when(step // each == number)(functools.partial(emit, tile_ref))


def prepare(pieces, order, spread):
    count, (each, k, size, _) = len(pieces), pieces[0].shape
    total = spread.shape[0]
    in_specs = [
        pl.BlockSpec((1, 1, size), lambda s, o: (o[s // each] * each + s % each, 0, 0))
    ]
    for number in range(count):
        in_specs.append(
            pl.BlockSpec(
                (1, k, size, size),
                lambda s, o, number=number: (jnp.clip(s - number * each, 0, each - 1), 0, 0, 0),
            )
        )
    return pl.pallas_call(
        functools.partial(prepare_body, count, each),
        grid_spec=pltpu.PrefetchScalarGridSpec(
            num_scalar_prefetch=1,
            grid=(count * each,),
            in_specs=in_specs,
            out_specs=pl.BlockSpec(memory_space=pltpu.VMEM),
        ),
        out_shape=pltpu.VMEM((total, 2 * size, k * size), BF16),
        compiler_params=params(),
        cost_estimate=pl.CostEstimate(
            flops=0, transcendentals=0, bytes_accessed=count * each * k * size * size * 8
        ),
        name="prepare",
    )(order, spread, *pieces)


def observe_body(steps, shards, groups, target_ref, row_ref, data_ref, *refs):
    tiles = refs[: sum(groups)]
    states = refs[len(tiles) : len(tiles) + steps * shards]
    out, seen_ref, gram_ref = refs[len(tiles) + len(states) :]
    size = out.shape[-1]
    members = size
    rows = steps * members
    all_rows = rows + MEAN_ROWS
    blocks = states[0].shape[-1] // size
    slot_row = lax.broadcasted_iota(jnp.int32, (MEAN_ROWS, size), 0)
    for mask in range(shards):
        first = (row_ref[0] ^ mask) * blocks
        for block in range(blocks):
            columns = slice(block * size, (block + 1) * size)
            means = jnp.zeros((MEAN_ROWS, size), F32)
            for i in range(steps):
                value = states[i * shards + mask][0, :, columns]
                mean = jnp.mean(value, axis=0, keepdims=True)
                high, low = split(value - mean)
                at = i * members
                seen_ref[first + block, at : at + members] = high
                seen_ref[first + block, all_rows + at : all_rows + at + members] = low
                means = jnp.where(slot_row == i, mean, means)
            high, low = split(means)
            seen_ref[first + block, rows:all_rows] = high
            seen_ref[first + block, all_rows + rows :] = low
    gram_ref[...] = jnp.zeros_like(gram_ref)
    nonzero = target_ref.shape[1]

    def visit(base, parts, at_once, step, _):
        seen = []
        for j in range(at_once):
            at = step * at_once + j
            left = jnp.concatenate(
                [seen_ref[target_ref[base + at, k]] for k in range(nonzero)], axis=1
            )
            right = jnp.concatenate([part[at] for part in parts], axis=1)
            both = by_rows(left, right)
            both = both[:all_rows] + both[all_rows:]
            seen.append(both[:, :size] + both[:, size:])
        for j in range(0, at_once, 2):
            two = seen[j : j + 2]
            at = base + step * at_once + j
            for i in range(steps):
                white = jnp.concatenate(
                    [value[i * members : (i + 1) * members] for value in two], axis=1
                )
                white_high, white_low = split(white)
                innovation = jnp.concatenate(
                    [
                        data_ref[i, at + n] - value[rows + i : rows + i + 1]
                        for n, value in enumerate(two)
                    ],
                    axis=1,
                )
                inn_high, inn_low = split(innovation)
                wide_row = lax.broadcasted_iota(jnp.int32, (MEAN_ROWS, len(two) * size), 0)
                extra = jnp.where(
                    wide_row == 0,
                    inn_high.astype(F32),
                    jnp.where(wide_row == 1, inn_low.astype(F32), 0.0),
                ).astype(BF16)
                gram_ref[i] += by_rows(
                    jnp.concatenate([white_high, extra], axis=0),
                    jnp.concatenate([white_high, white_low], axis=0),
                )
        return 0

    base, start = 0, 0
    for group in groups:
        parts = tiles[start : start + group]
        count = parts[0].shape[0]
        at_once = min(4, count)
        lax.fori_loop(
            0, count // at_once, functools.partial(visit, base, parts, at_once), 0
        )
        base, start = base + count, start + group
    for i in range(steps):
        total = gram_ref[i]
        cross = total[:members, members:]
        out[i, :members] = total[:members, :members] + cross + jnp.transpose(cross)
        vector = (
            total[members : members + 1, :members]
            + total[members : members + 1, members:]
            + total[members + 1 : members + 2, :members]
        )
        out[i, members:] = jnp.broadcast_to(vector, (8, members))


def observe(chunk, states, tile_groups, targets, data, row):
    steps, shards = len(chunk), len(states[0])
    tiles = [part for group in tile_groups for part in group]
    _, double, _ = tiles[0].shape
    size = double // 2
    members = size
    columns = states[0][0][0].shape[-1]
    vmem = pl.BlockSpec(memory_space=pltpu.VMEM)
    smem = pl.BlockSpec(memory_space=pltpu.SMEM)
    in_specs = [smem, smem, vmem] + [vmem] * len(tiles)
    flat = []
    for pieces in states:
        for piece, g in pieces:
            flat.append(piece)
            in_specs.append(
                pl.BlockSpec(
                    (1, members, columns), lambda s, g=g: (g, 0, 0), pipeline_mode=pl.Buffered(1)
                )
            )
    slots = shards * (columns // size)
    rows = steps * members + MEAN_ROWS
    total, nonzero = targets.shape
    return pl.pallas_call(
        functools.partial(observe_body, steps, shards, [len(group) for group in tile_groups]),
        grid=(1,),
        in_specs=in_specs,
        out_specs=pl.BlockSpec((steps, members + 8, members), lambda s: (0, 0, 0)),
        scratch_shapes=[
            pltpu.VMEM((slots, 2 * rows, size), BF16),
            pltpu.VMEM((steps, members + MEAN_ROWS, 2 * members), F32),
        ],
        out_shape=jax.ShapeDtypeStruct((steps, members + 8, members), F32),
        compiler_params=params(),
        cost_estimate=pl.CostEstimate(
            flops=2 * 4 * rows * size * nonzero * size * total,
            transcendentals=0,
            bytes_accessed=total * double * nonzero * size * 2,
        ),
        name="observe",
    )(targets, row, data, *tiles, *flat)


def roots(info_and_vectors, inflations, size):
    identity = eye(size)
    info = [value[:size] + identity for value in info_and_vectors]
    vector = [value[size:] for value in info_and_vectors]
    bound = [
        jnp.max(jnp.sum(jnp.abs(value), axis=1, keepdims=True), axis=0, keepdims=True)
        for value in info
    ]
    scaled = [value / top for value, top in zip(info, bound)]
    update = [1.5 * identity - 0.5 * value for value in scaled]
    inverse = update
    root = [product(value, up) for value, up in zip(scaled, update)]
    for number in range(1, NS_ITERS):
        update = [1.5 * identity - 0.5 * product(q, y) for q, y in zip(inverse, root)]
        if number < NS_ITERS - 1:
            root = [product(y, up) for y, up in zip(root, update)]
        inverse = [product(up, q) for q, up in zip(inverse, update)]
    matrices = []
    for i, inflation in enumerate(inflations):
        half_root = inverse[i] / jnp.sqrt(bound[i])
        half = lax.dot_general(
            vector[i],
            half_root,
            (((1,), (1,)), ((), ())),
            precision=exact_product,
            preferred_element_type=F32,
        )
        weights = jnp.sum(half_root * half[:1], axis=1, keepdims=True)
        mixing = weights + inflation * half_root
        mixing = mixing - jnp.mean(mixing, axis=0, keepdims=True)
        matrices.append(mixing + 1.0 / size)
    return matrices


def transform_body(steps, parts, inflation_ref, *refs):
    ins, out = refs[:parts], refs[parts]
    sums = [sum((ref[i] for ref in ins[1:]), ins[0][i]) for i in range(steps)]
    inflations = [inflation_ref[i] for i in range(steps)]
    for i, matrix in enumerate(roots(sums, inflations, out.shape[-1])):
        out[i] = matrix


def transforms(parts, inflation):
    steps, _, members = parts[0].shape
    vmem = pl.BlockSpec(memory_space=pltpu.VMEM)
    return pl.pallas_call(
        functools.partial(transform_body, steps, len(parts)),
        in_specs=[pl.BlockSpec(memory_space=pltpu.SMEM)] + [vmem] * len(parts),
        out_specs=vmem,
        out_shape=jax.ShapeDtypeStruct((steps, members, members), F32),
        compiler_params=params(),
        cost_estimate=pl.CostEstimate(
            flops=steps * 21 * 6 * 2 * members**3 * 4,
            transcendentals=0,
            bytes_accessed=steps * members * members * 12,
        ),
        name="transforms",
    )(inflation, *parts)


def close_body(steps, parts, low_ref, inflation_ref, *refs):
    mine, other = refs[:parts], refs[parts : 2 * parts]
    running_ref, suffix_ref, matrix_ref = refs[2 * parts :]
    even = low_ref[0] == 0
    sums = [sum((ref[i] for ref in mine[1:]), mine[0][i]) for i in range(steps)]
    sums += [sum((ref[i] for ref in other[1:]), other[0][i]) for i in range(steps)]
    ordered, inflations = [], []
    for i in range(steps):
        ordered.append(jnp.where(even, sums[i], sums[steps + i]))
        ordered.append(jnp.where(even, sums[steps + i], sums[i]))
        inflations += [inflation_ref[2 * i], inflation_ref[2 * i + 1]]
    matrices = roots(ordered, inflations, suffix_ref.shape[-1])
    running = running_ref[0]
    for i in reversed(range(2 * steps)):
        matrix_ref[i] = matrices[i]
        running = product(matrices[i], running)
        suffix_ref[i] = running


def close(mine, other, running, inflation, low):
    steps, _, members = mine[0].shape
    vmem = pl.BlockSpec(memory_space=pltpu.VMEM)
    smem = pl.BlockSpec(memory_space=pltpu.SMEM)
    return pl.pallas_call(
        functools.partial(close_body, steps, len(mine)),
        in_specs=[smem, smem] + [vmem] * (2 * len(mine) + 1),
        out_specs=(vmem, vmem),
        out_shape=(jax.ShapeDtypeStruct((2 * steps, members, members), F32),) * 2,
        compiler_params=params(),
        cost_estimate=pl.CostEstimate(
            flops=steps * 2 * 21 * 6 * 2 * members**3 * 4,
            transcendentals=0,
            bytes_accessed=steps * members * members * 24,
        ),
        name="close",
    )(low, inflation, *mine, *other, running)


def chain_body(steps, first, low_ref, *refs):
    mine, other = refs[:2]
    out = refs[-1]
    running = None if first else refs[2][0]
    even = low_ref[0] == 0
    for i in reversed(range(steps)):
        earlier = jnp.where(even, mine[i], other[i])
        later = jnp.where(even, other[i], mine[i])
        after = later if running is None else product(later, running)
        out[2 * i + 1] = after
        running = product(earlier, after)
        out[2 * i] = running


def chain(mine, other, running, low):
    steps, size, _ = mine.shape
    vmem = pl.BlockSpec(memory_space=pltpu.VMEM)
    args = [mine, other] + ([] if running is None else [running])
    return pl.pallas_call(
        functools.partial(chain_body, steps, running is None),
        in_specs=[pl.BlockSpec(memory_space=pltpu.SMEM)] + [vmem] * len(args),
        out_specs=vmem,
        out_shape=jax.ShapeDtypeStruct((2 * steps, size, size), F32),
        compiler_params=params(),
        cost_estimate=pl.CostEstimate(
            flops=steps * 2 * 6 * 2 * size**3 * 8, transcendentals=0,
            bytes_accessed=steps * size * size * 16,
        ),
        name="chain",
    )(low, *args)


def couple_body(core_ref, mine, other, out):
    first = core_ref[0] == 0
    out[...] = product(
        jnp.where(first, mine[...], other[...]), jnp.where(first, other[...], mine[...])
    )


def couple(mine, other, core):
    vmem = pl.BlockSpec(memory_space=pltpu.VMEM)
    return pl.pallas_call(
        couple_body,
        in_specs=[pl.BlockSpec(memory_space=pltpu.SMEM), vmem, vmem],
        out_specs=vmem,
        out_shape=jax.ShapeDtypeStruct(mine.shape, F32),
        compiler_params=params(),
        name="couple",
    )(core, mine, other)


def weigh(weights, state_ref, out_ref):
    high, low = split(jnp.transpose(weights))
    state_high, state_low = split(state_ref[0])
    out_ref[0] = jnp.dot(
        jnp.concatenate([high, high], axis=1),
        jnp.concatenate([state_high, state_low], axis=0),
        preferred_element_type=F32,
    ) + jnp.dot(low, state_high, preferred_element_type=F32)


def filtered(weights, prior):
    steps, members, columns = prior.shape

    def body(weights_ref, state_ref, out_ref):
        weigh(weights_ref[0], state_ref, out_ref)

    return pl.pallas_call(
        body,
        grid=(steps,),
        in_specs=[
            pl.BlockSpec((1, members, members), lambda t: (t, 0, 0)),
            pl.BlockSpec((1, members, columns), lambda t: (t, 0, 0)),
        ],
        out_specs=pl.BlockSpec((1, members, columns), lambda t: (t, 0, 0)),
        out_shape=jax.ShapeDtypeStruct(prior.shape, F32),
        compiler_params=params(),
        cost_estimate=pl.CostEstimate(
            flops=steps * 3 * 2 * members * members * columns,
            transcendentals=0,
            bytes_accessed=prior.size * 8,
        ),
        name="filtered",
    )(weights, prior)


def smooth_body(groups, place_ref, suffix_ref, state_ref, partner_ref, *refs):
    later, out_ref, end_ref = refs[: groups - 1], refs[-2], refs[-1]
    size = suffix_ref.shape[-1]

    @pl.when(pl.program_id(0) == 0)
    def _():
        identity = eye(size)
        chain = [jnp.where(place_ref[1] == 0, partner_ref[...], identity)]
        for ahead, ref in enumerate(later, 1):
            chain.append(jnp.where(place_ref[0] + ahead < groups, ref[...], identity))
        while len(chain) > 1:
            joined = [product(a, b) for a, b in zip(chain[::2], chain[1::2])]
            chain = joined + ([chain[-1]] if len(chain) % 2 else [])
        end_ref[...] = chain[0]

    weigh(product(suffix_ref[0], end_ref[...]), state_ref, out_ref)


def smoothed(suffix, prior, partner, later, place):
    steps, members, columns = prior.shape
    groups = len(later) + 1
    vmem = pl.BlockSpec((members, members), lambda t: (0, 0))
    return pl.pallas_call(
        functools.partial(smooth_body, groups),
        grid=(steps,),
        in_specs=[
            pl.BlockSpec(memory_space=pltpu.SMEM),
            pl.BlockSpec((1, members, members), lambda t: (t, 0, 0)),
            pl.BlockSpec((1, members, columns), lambda t: (t, 0, 0)),
        ]
        + [vmem] * groups,
        out_specs=pl.BlockSpec((1, members, columns), lambda t: (t, 0, 0)),
        out_shape=jax.ShapeDtypeStruct(prior.shape, F32),
        scratch_shapes=[pltpu.VMEM((members, members), F32)],
        compiler_params=params(),
        cost_estimate=pl.CostEstimate(
            flops=steps * 3 * 2 * members * members * columns, transcendentals=0,
            bytes_accessed=prior.size * 8,
        ),
        name="smoothed",
    )(place, suffix, prior, partner, *later)


def exchange(value, axis, bit):
    count = lax.axis_size(axis)
    return lax.ppermute(value, axis, [(i, i ^ bit) for i in range(count)])


def smoother(
    prior_ensemble,
    observation_data,
    inverse_error_spread,
    anomaly_inflation,
    nonzero_tiles,
    nonzero_tile_targets,
):
    steps, members, columns = prior_ensemble.shape
    block_rows, nonzero, size, _ = nonzero_tiles.shape
    shards = lax.axis_size("row")
    row, place = lax.axis_index("row"), lax.axis_index("tm")
    low, core = row & 1, place & 1
    pairs = steps // 2
    early, last = ((2, 3), (1,)), (0,)
    chunks = early + (last,)
    sequence = [g for chunk in chunks for g in reversed(chunk)]
    bits = []
    while 2 << len(bits) < shards:
        bits.append(2 << len(bits))

    spread = inverse_error_spread / float(members - 1) ** 0.5
    data = observation_data * spread
    halves = data.reshape(pairs, 2, -1)
    of_low = functools.partial(lax.dynamic_index_in_dim, axis=1, keepdims=False)
    padded = jnp.zeros((data.shape[1],), F32)
    padded = padded.at[: nonzero_tile_targets.size].set(nonzero_tile_targets.reshape(-1).astype(F32))
    note = jnp.concatenate([of_low(halves, 1 - low), spread[None], padded[None]], axis=0)
    quarter = place & 3
    each = block_rows // 4
    middle = nonzero // 2
    note = exchange(note, "row", 1)
    fetched = []
    for half in range(2):
        group = lax.dynamic_slice(
            nonzero_tiles,
            (quarter * each, half * middle, 0, 0),
            (each, middle, size, size),
        )
        fetched.append(exchange(group, "row", 1))
    states = prior_ensemble.reshape(pairs, 2, members, columns)
    mine, theirs = of_low(states, low), of_low(states, 1 - low)
    sent = {g: exchange(theirs[g : g + 1], "row", 1) for g in sequence}
    own_moved = {bit: exchange(mine, "row", bit) for bit in bits}
    pieces = {}
    for g in sequence:
        have = [(mine, g), (sent[g], 0)]
        for bit in bits:
            moved = [(own_moved[bit], g)]
            for value, at in have[1:]:
                moved.append((exchange(value[at : at + 1], "row", bit), 0))
            have = have + moved
        pieces[g] = have

    per_row = spread.reshape(block_rows, 1, size)
    own_tiles = prepare([nonzero_tiles], jnp.zeros((1,), jnp.int32), per_row)
    their_data = note[:pairs].reshape(pairs, block_rows, 1, size)
    own_data = of_low(halves, low).reshape(pairs, block_rows, 1, size)
    all_data = jnp.concatenate([own_data, their_data], axis=1)
    their_spread = note[pairs].reshape(block_rows, 1, size)
    their_targets = note[pairs + 1, : nonzero_tile_targets.size].astype(jnp.int32)
    targets = jnp.concatenate(
        [nonzero_tile_targets, their_targets.reshape(block_rows, nonzero)], axis=0
    )
    order = jnp.stack([quarter, quarter ^ 2, quarter ^ 1, quarter ^ 3]).astype(jnp.int32)
    their_tiles = []
    for value in fetched:
        across = exchange(value, "tm", 2)
        beside = exchange(value, "tm", 1)
        parts = [value, across, beside, exchange(across, "tm", 1)]
        their_tiles.append(prepare(parts, order, their_spread))
    tile_groups = [[own_tiles], their_tiles]

    row_scalar = row.astype(jnp.int32).reshape(1)
    low_scalar = low.astype(jnp.int32).reshape(1)
    inflation = of_low(anomaly_inflation.reshape(pairs, 2), low)

    def observed(chunk):
        part = observe(
            chunk,
            [pieces[g] for g in chunk],
            tile_groups,
            targets,
            all_data[chunk[0] : chunk[0] + len(chunk)],
            row_scalar,
        )
        for bit in bits[:-1]:
            part = part + exchange(part, "row", bit)
        return part

    running, suffix, matrices = None, [None] * pairs, [None] * pairs
    for chunk in early:
        part = observed(chunk)
        parts = [part] + [exchange(part, "row", bit) for bit in bits[-1:]]
        matrix = transforms(parts, inflation[chunk[0] : chunk[0] + len(chunk)])
        other = exchange(matrix, "row", 1)
        products = chain(matrix, other, running, low_scalar)
        running = products[:1]
        even = jnp.where(low == 0, matrix, other)
        odd = jnp.where(low == 0, other, matrix)
        both = jnp.stack([even, odd], axis=1)
        for number, g in enumerate(chunk):
            suffix[g] = products[2 * number : 2 * number + 2]
            matrices[g] = both[number]
    part = observed(last)
    own_parts, other_parts = [part], [exchange(part, "row", 1)]
    for bit in bits[-1:]:
        own_parts.append(exchange(part, "row", bit))
        other_parts.append(exchange(part, "row", bit | 1))
    products, both = close(
        own_parts, other_parts, running, anomaly_inflation[: 2 * len(last)], low_scalar
    )
    whole = products[0]
    suffix[0], matrices[0] = products, both

    core_scalar = core.astype(jnp.int32).reshape(1)
    partner = exchange(whole, "tm", 1)
    coupled = couple(whole, partner, core_scalar)
    groups = lax.axis_size("tm") // 2
    later = []
    for ahead in range(1, groups):
        hop = 2 * ahead
        later.append(lax.ppermute(coupled, "tm", [(i + hop, i) for i in range(2 * groups - hop)]))
    filtered_ensemble = filtered(jnp.concatenate(matrices), prior_ensemble)
    where = jnp.stack([place // 2, core]).astype(jnp.int32)
    smoothed_ensemble = smoothed(
        jnp.concatenate(suffix), prior_ensemble, partner, later, where
    )
    return (smoothed_ensemble, filtered_ensemble)


def solution(mesh):
    placed = (
        P("tm", None, "row"),
        P("tm", "row"),
        P("row"),
        P("tm"),
        P("row", None, None, None),
        P("row", None),
    )
    return jax.shard_map(
        smoother,
        mesh=mesh,
        in_specs=placed,
        out_specs=(P("tm", None, "row"), P("tm", None, "row")),
        check_vma=False,
    )
```

```python
import functools

import jax
import jax.numpy as jnp
from jax import lax
from jax.experimental import pallas as pl
from jax.experimental.pallas import tpu as pltpu
from jax.sharding import PartitionSpec as P


NS_ITERS = 8
F32, BF16 = jnp.float32, jnp.bfloat16
exact_product = lax.Precision.HIGHEST
MEAN_ROWS = 16


def split(value):
    high = value.astype(BF16)
    return high, (value - high.astype(F32)).astype(BF16)


def product(left, right):
    return jnp.dot(left, right, precision=exact_product, preferred_element_type=F32)


def by_rows(left, right):
    return lax.dot_general(left, right, (((1,), (1,)), ((), ())), preferred_element_type=F32)


def eye(size):
    rows = lax.broadcasted_iota(jnp.int32, (size, size), 0)
    columns = lax.broadcasted_iota(jnp.int32, (size, size), 1)
    return (rows == columns).astype(F32)


def params(limit):
    return pltpu.CompilerParams(vmem_limit_bytes=limit << 20)


def prepare_body(count, order_ref, spread_ref, *refs):
    tiles, out = refs[:count], refs[-1]
    size = spread_ref.shape[-1]
    for number, tile_ref in enumerate(tiles):
        each = tile_ref.shape[0]

        def emit(row, _):
            at = order_ref[number] * each + row
            scale = jnp.transpose(jnp.broadcast_to(spread_ref[at], (size, size)))
            for k in range(tile_ref.shape[1]):
                high, low = split(tile_ref[row, k] * scale)
                out[at, :size, k * size : (k + 1) * size] = high
                out[at, size:, k * size : (k + 1) * size] = low
            return 0

        lax.fori_loop(0, each, emit, 0)


def prepare(pieces, order, spread):
    count, (each, k, size, _) = len(pieces), pieces[0].shape
    total = spread.shape[0]
    vmem = pl.BlockSpec(memory_space=pltpu.VMEM)
    return pl.pallas_call(
        functools.partial(prepare_body, count),
        in_specs=[pl.BlockSpec(memory_space=pltpu.SMEM), vmem] + [vmem] * count,
        out_specs=vmem,
        out_shape=pltpu.VMEM((total, 2 * size, k * size), BF16),
        compiler_params=params(10),
        cost_estimate=pl.CostEstimate(
            flops=0, transcendentals=0, bytes_accessed=count * each * k * size * size * 8
        ),
        name="prepare",
    )(order, spread, *pieces)


def observe_body(steps, shards, groups, places, target_ref, row_ref, data_ref, *refs):
    tiles = refs[: sum(groups)]
    states = refs[len(tiles) : len(tiles) + steps * shards]
    out, seen_ref, gram_ref = refs[len(tiles) + len(states) :]
    size = out.shape[-1]
    members = size
    rows = steps * members
    all_rows = rows + MEAN_ROWS
    blocks = states[0].shape[-1] // size
    slot_row = lax.broadcasted_iota(jnp.int32, (MEAN_ROWS, size), 0)
    for mask in range(shards):
        first = (row_ref[0] ^ mask) * blocks
        for block in range(blocks):
            columns = slice(block * size, (block + 1) * size)
            means = jnp.zeros((MEAN_ROWS, size), F32)
            for i in range(steps):
                value = states[i * shards + mask][places[i * shards + mask], :, columns]
                mean = jnp.mean(value, axis=0, keepdims=True)
                high, low = split(value - mean)
                at = i * members
                seen_ref[first + block, at : at + members] = high
                seen_ref[first + block, all_rows + at : all_rows + at + members] = low
                means = jnp.where(slot_row == i, mean, means)
            high, low = split(means)
            seen_ref[first + block, rows:all_rows] = high
            seen_ref[first + block, all_rows + rows :] = low
    gram_ref[...] = jnp.zeros_like(gram_ref)
    nonzero = target_ref.shape[1]

    def visit(base, parts, at_once, step, _):
        seen = []
        for j in range(at_once):
            at = step * at_once + j
            left = jnp.concatenate(
                [seen_ref[target_ref[base + at, k]] for k in range(nonzero)], axis=1
            )
            right = jnp.concatenate([part[at] for part in parts], axis=1)
            both = by_rows(left, right)
            both = both[:all_rows] + both[all_rows:]
            seen.append(both[:, :size] + both[:, size:])
        for j in range(0, at_once, 2):
            two = seen[j : j + 2]
            at = base + step * at_once + j
            for i in range(steps):
                white = jnp.concatenate(
                    [value[i * members : (i + 1) * members] for value in two], axis=1
                )
                white_high, white_low = split(white)
                innovation = jnp.concatenate(
                    [
                        data_ref[i, at + n] - value[rows + i : rows + i + 1]
                        for n, value in enumerate(two)
                    ],
                    axis=1,
                )
                inn_high, inn_low = split(innovation)
                wide_row = lax.broadcasted_iota(jnp.int32, (MEAN_ROWS, len(two) * size), 0)
                extra = jnp.where(
                    wide_row == 0,
                    inn_high.astype(F32),
                    jnp.where(wide_row == 1, inn_low.astype(F32), 0.0),
                ).astype(BF16)
                gram_ref[i] += by_rows(
                    jnp.concatenate([white_high, extra], axis=0),
                    jnp.concatenate([white_high, white_low], axis=0),
                )
        return 0

    base, start = 0, 0
    for group in groups:
        parts = tiles[start : start + group]
        count = parts[0].shape[0]
        at_once = min(8, count)
        lax.fori_loop(
            0, count // at_once, functools.partial(visit, base, parts, at_once), 0
        )
        base, start = base + count, start + group
    for i in range(steps):
        total = gram_ref[i]
        cross = total[:members, members:]
        out[i, :members] = total[:members, :members] + cross + jnp.transpose(cross)
        vector = (
            total[members : members + 1, :members]
            + total[members : members + 1, members:]
            + total[members + 1 : members + 2, :members]
        )
        out[i, members:] = jnp.broadcast_to(vector, (8, members))


def observe(chunk, states, tile_groups, targets, data, row):
    steps, shards = len(chunk), len(states[0])
    tiles = [part for group in tile_groups for part in group]
    _, double, _ = tiles[0].shape
    size = double // 2
    members = size
    columns = states[0][0][0].shape[-1]
    places = [g for pieces in states for _, g in pieces]
    flat = [piece for pieces in states for piece, _ in pieces]
    vmem = pl.BlockSpec(memory_space=pltpu.VMEM)
    smem = pl.BlockSpec(memory_space=pltpu.SMEM)
    in_specs = [smem, smem, vmem] + [vmem] * (len(tiles) + len(flat))
    slots = shards * (columns // size)
    rows = steps * members + MEAN_ROWS
    total, nonzero = targets.shape
    groups = [len(group) for group in tile_groups]
    return pl.pallas_call(
        functools.partial(observe_body, steps, shards, groups, places),
        in_specs=in_specs,
        out_specs=vmem,
        scratch_shapes=[
            pltpu.VMEM((slots, 2 * rows, size), BF16),
            pltpu.VMEM((steps, members + MEAN_ROWS, 2 * members), F32),
        ],
        out_shape=jax.ShapeDtypeStruct((steps, members + 8, members), F32),
        compiler_params=params(18),
        cost_estimate=pl.CostEstimate(
            flops=2 * 4 * rows * size * nonzero * size * total,
            transcendentals=0,
            bytes_accessed=total * double * nonzero * size * 2,
        ),
        name="observe",
    )(targets, row, data, *tiles, *flat)


def roots(info_and_vectors, inflations, size):
    identity = eye(size)
    info = [value[:size] + identity for value in info_and_vectors]
    vector = [value[size:] for value in info_and_vectors]
    bound = [
        jnp.max(jnp.sum(jnp.abs(value), axis=1, keepdims=True), axis=0, keepdims=True)
        for value in info
    ]
    scaled = [value / top for value, top in zip(info, bound)]
    update = [1.5 * identity - 0.5 * value for value in scaled]
    inverse = update
    root = [product(value, up) for value, up in zip(scaled, update)]
    for number in range(1, NS_ITERS):
        update = [1.5 * identity - 0.5 * product(q, y) for q, y in zip(inverse, root)]
        if number < NS_ITERS - 1:
            root = [product(y, up) for y, up in zip(root, update)]
        inverse = [product(up, q) for q, up in zip(inverse, update)]
    matrices = []
    for i, inflation in enumerate(inflations):
        half_root = inverse[i] / jnp.sqrt(bound[i])
        half = lax.dot_general(
            vector[i],
            half_root,
            (((1,), (1,)), ((), ())),
            precision=exact_product,
            preferred_element_type=F32,
        )
        weights = jnp.sum(half_root * half[:1], axis=1, keepdims=True)
        mixing = weights + inflation * half_root
        mixing = mixing - jnp.mean(mixing, axis=0, keepdims=True)
        matrices.append(mixing + 1.0 / size)
    return matrices


def transform_body(parts, inflation_ref, *refs):
    ins, out = refs[:-1], refs[-1]
    sums = []
    for start in range(0, len(ins), parts):
        group = ins[start : start + parts]
        for i in range(group[0].shape[0]):
            sums.append(sum((ref[i] for ref in group[1:]), group[0][i]))
    inflations = [inflation_ref[i] for i in range(len(sums))]
    for i, matrix in enumerate(roots(sums, inflations, out.shape[-1])):
        out[i] = matrix


def transforms(groups, inflation):
    parts = len(groups[0])
    flat = [part for group in groups for part in group]
    steps, members = sum(group[0].shape[0] for group in groups), flat[0].shape[-1]
    vmem = pl.BlockSpec(memory_space=pltpu.VMEM)
    return pl.pallas_call(
        functools.partial(transform_body, parts),
        in_specs=[pl.BlockSpec(memory_space=pltpu.SMEM)] + [vmem] * len(flat),
        out_specs=vmem,
        out_shape=jax.ShapeDtypeStruct((steps, members, members), F32),
        compiler_params=params(8),
        cost_estimate=pl.CostEstimate(
            flops=steps * 21 * 6 * 2 * members**3 * 4,
            transcendentals=0,
            bytes_accessed=steps * members * members * 12,
        ),
        name="transforms",
    )(inflation, *flat)


def close_body(steps, parts, low_ref, inflation_ref, *refs):
    mine, other = refs[:parts], refs[parts : 2 * parts]
    (matrix_ref,) = refs[2 * parts :]
    even = low_ref[0] == 0
    sums = [sum((ref[i] for ref in mine[1:]), mine[0][i]) for i in range(steps)]
    sums += [sum((ref[i] for ref in other[1:]), other[0][i]) for i in range(steps)]
    ordered, inflations = [], []
    for i in range(steps):
        ordered.append(jnp.where(even, sums[i], sums[steps + i]))
        ordered.append(jnp.where(even, sums[steps + i], sums[i]))
        inflations += [inflation_ref[2 * i], inflation_ref[2 * i + 1]]
    for i, matrix in enumerate(roots(ordered, inflations, matrix_ref.shape[-1])):
        matrix_ref[i] = matrix


def close(mine, other, inflation, low):
    steps, _, members = mine[0].shape
    vmem = pl.BlockSpec(memory_space=pltpu.VMEM)
    smem = pl.BlockSpec(memory_space=pltpu.SMEM)
    return pl.pallas_call(
        functools.partial(close_body, steps, len(mine)),
        in_specs=[smem, smem] + [vmem] * (2 * len(mine)),
        out_specs=vmem,
        out_shape=jax.ShapeDtypeStruct((2 * steps, members, members), F32),
        compiler_params=params(8),
        cost_estimate=pl.CostEstimate(
            flops=steps * 2 * 21 * 6 * 2 * members**3 * 4,
            transcendentals=0,
            bytes_accessed=steps * members * members * 24,
        ),
        name="close",
    )(low, inflation, *mine, *other)


def chain_body(steps, low_ref, first_ref, mine, other, out, all_ref):
    running, early = None, first_ref.shape[0]
    even = low_ref[0] == 0
    for i in reversed(range(steps)):
        for matrix, at in (
            (jnp.where(even, other[i], mine[i]), early + 2 * i + 1),
            (jnp.where(even, mine[i], other[i]), early + 2 * i),
        ):
            all_ref[at] = matrix
            running = matrix if running is None else product(matrix, running)
            out[at] = running
    for i in reversed(range(early)):
        all_ref[i] = first_ref[i]
        running = product(first_ref[i], running)
        out[i] = running


def chain(first, mine, other, low):
    steps, size, _ = mine.shape
    total = first.shape[0] + 2 * steps
    vmem = pl.BlockSpec(memory_space=pltpu.VMEM)
    return pl.pallas_call(
        functools.partial(chain_body, steps),
        in_specs=[pl.BlockSpec(memory_space=pltpu.SMEM)] + [vmem] * 3,
        out_specs=(vmem, vmem),
        out_shape=(jax.ShapeDtypeStruct((total, size, size), F32),) * 2,
        compiler_params=params(6),
        cost_estimate=pl.CostEstimate(
            flops=total * 6 * 2 * size**3 * 8,
            transcendentals=0,
            bytes_accessed=total * size * size * 16,
        ),
        name="chain",
    )(low, first, mine, other)


def couple_body(core_ref, mine, other, out):
    first = core_ref[0] == 0
    out[...] = product(
        jnp.where(first, mine[...], other[...]), jnp.where(first, other[...], mine[...])
    )


def couple(mine, other, core):
    vmem = pl.BlockSpec(memory_space=pltpu.VMEM)
    return pl.pallas_call(
        couple_body,
        in_specs=[pl.BlockSpec(memory_space=pltpu.SMEM), vmem, vmem],
        out_specs=vmem,
        out_shape=jax.ShapeDtypeStruct(mine.shape, F32),
        compiler_params=params(4),
        name="couple",
    )(core, mine, other)


def weigh(weights, state_ref, out_ref):
    high, low = split(jnp.transpose(weights))
    state_high, state_low = split(state_ref[0])
    out_ref[0] = jnp.dot(
        jnp.concatenate([high, high], axis=1),
        jnp.concatenate([state_high, state_low], axis=0),
        preferred_element_type=F32,
    ) + jnp.dot(low, state_high, preferred_element_type=F32)


def filtered(weights, prior):
    steps, members, columns = prior.shape

    def body(weights_ref, state_ref, out_ref):
        weigh(weights_ref[0], state_ref, out_ref)

    return pl.pallas_call(
        body,
        grid=(steps,),
        in_specs=[
            pl.BlockSpec((1, members, members), lambda t: (t, 0, 0)),
            pl.BlockSpec((1, members, columns), lambda t: (t, 0, 0)),
        ],
        out_specs=pl.BlockSpec((1, members, columns), lambda t: (t, 0, 0)),
        out_shape=jax.ShapeDtypeStruct(prior.shape, F32),
        compiler_params=params(8),
        cost_estimate=pl.CostEstimate(
            flops=steps * 3 * 2 * members * members * columns,
            transcendentals=0,
            bytes_accessed=prior.size * 8,
        ),
        name="filtered",
    )(weights, prior)


def smooth_body(groups, place_ref, suffix_ref, state_ref, partner_ref, *refs):
    later, out_ref, end_ref = refs[: groups - 1], refs[-2], refs[-1]
    size = suffix_ref.shape[-1]

    @pl.when(pl.program_id(0) == 0)
    def _():
        identity = eye(size)
        chain = [jnp.where(place_ref[1] == 0, partner_ref[...], identity)]
        for ahead, ref in enumerate(later, 1):
            chain.append(jnp.where(place_ref[0] + ahead < groups, ref[...], identity))
        while len(chain) > 1:
            joined = [product(a, b) for a, b in zip(chain[::2], chain[1::2])]
            chain = joined + ([chain[-1]] if len(chain) % 2 else [])
        end_ref[...] = chain[0]

    weigh(product(suffix_ref[0], end_ref[...]), state_ref, out_ref)


def smoothed(suffix, prior, partner, later, place):
    steps, members, columns = prior.shape
    groups = len(later) + 1
    vmem = pl.BlockSpec((members, members), lambda t: (0, 0))
    return pl.pallas_call(
        functools.partial(smooth_body, groups),
        grid=(steps,),
        in_specs=[
            pl.BlockSpec(memory_space=pltpu.SMEM),
            pl.BlockSpec((1, members, members), lambda t: (t, 0, 0)),
            pl.BlockSpec((1, members, columns), lambda t: (t, 0, 0)),
        ]
        + [vmem] * groups,
        out_specs=pl.BlockSpec((1, members, columns), lambda t: (t, 0, 0)),
        out_shape=jax.ShapeDtypeStruct(prior.shape, F32),
        scratch_shapes=[pltpu.VMEM((members, members), F32)],
        compiler_params=params(10),
        cost_estimate=pl.CostEstimate(
            flops=steps * 3 * 2 * members * members * columns, transcendentals=0,
            bytes_accessed=prior.size * 8,
        ),
        name="smoothed",
    )(place, suffix, prior, partner, *later)


def exchange(value, axis, bit):
    count = lax.axis_size(axis)
    return lax.ppermute(value, axis, [(i, i ^ bit) for i in range(count)])


def smoother(
    prior_ensemble,
    observation_data,
    inverse_error_spread,
    anomaly_inflation,
    nonzero_tiles,
    nonzero_tile_targets,
):
    steps, members, columns = prior_ensemble.shape
    block_rows, nonzero, size, _ = nonzero_tiles.shape
    shards = lax.axis_size("row")
    row, place = lax.axis_index("row"), lax.axis_index("tm")
    low, core = row & 1, place & 1
    pairs = steps // 2
    early, last = ((2, 3), (1,)), (0,)
    chunks = early + (last,)
    sequence = [g for chunk in chunks for g in reversed(chunk)]
    bits = []
    while 2 << len(bits) < shards:
        bits.append(2 << len(bits))

    spread = inverse_error_spread / float(members - 1) ** 0.5
    data = observation_data * spread
    halves = data.reshape(pairs, 2, -1)
    of_low = functools.partial(lax.dynamic_index_in_dim, axis=1, keepdims=False)
    padded = jnp.zeros((data.shape[1],), F32)
    padded = padded.at[: nonzero_tile_targets.size].set(nonzero_tile_targets.reshape(-1).astype(F32))
    note = jnp.concatenate([of_low(halves, 1 - low), spread[None], padded[None]], axis=0)
    quarter = place & 3
    each = block_rows // 4
    middle = nonzero // 2
    note = exchange(note, "row", 1)
    fetched = []
    for half in range(2):
        group = lax.dynamic_slice(
            nonzero_tiles,
            (quarter * each, half * middle, 0, 0),
            (each, middle, size, size),
        )
        fetched.append(exchange(group, "row", 1))
    states = prior_ensemble.reshape(pairs, 2, members, columns)
    mine, theirs = of_low(states, low), of_low(states, 1 - low)
    sent = {g: exchange(theirs[g : g + 1], "row", 1) for g in sequence}
    own_moved = {bit: exchange(mine, "row", bit) for bit in bits}
    pieces = {}
    for g in sequence:
        have = [(mine, g), (sent[g], 0)]
        for bit in bits:
            moved = [(own_moved[bit], g)]
            for value, at in have[1:]:
                moved.append((exchange(value[at : at + 1], "row", bit), 0))
            have = have + moved
        pieces[g] = have

    per_row = spread.reshape(block_rows, 1, size)
    own_tiles = prepare([nonzero_tiles], jnp.zeros((1,), jnp.int32), per_row)
    their_data = note[:pairs].reshape(pairs, block_rows, 1, size)
    own_data = of_low(halves, low).reshape(pairs, block_rows, 1, size)
    all_data = jnp.concatenate([own_data, their_data], axis=1)
    their_spread = note[pairs].reshape(block_rows, 1, size)
    their_targets = note[pairs + 1, : nonzero_tile_targets.size].astype(jnp.int32)
    targets = jnp.concatenate(
        [nonzero_tile_targets, their_targets.reshape(block_rows, nonzero)], axis=0
    )
    order = jnp.stack([quarter, quarter ^ 2, quarter ^ 1, quarter ^ 3]).astype(jnp.int32)
    their_tiles = []
    for value in fetched:
        across = exchange(value, "tm", 2)
        beside = exchange(value, "tm", 1)
        parts = [value, across, beside, exchange(across, "tm", 1)]
        their_tiles.append(prepare(parts, order, their_spread))
    tile_groups = [[own_tiles], their_tiles]

    row_scalar = row.astype(jnp.int32).reshape(1)
    low_scalar = low.astype(jnp.int32).reshape(1)
    inflation = of_low(anomaly_inflation.reshape(pairs, 2), low)

    def observed(chunk):
        part = observe(
            chunk,
            [pieces[g] for g in chunk],
            tile_groups,
            targets,
            all_data[chunk[0] : chunk[0] + len(chunk)],
            row_scalar,
        )
        for bit in bits[:-1]:
            part = part + exchange(part, "row", bit)
        return part

    groups = []
    for chunk in early:
        part = observed(chunk)
        parts = [part] + [exchange(part, "row", bit) for bit in bits[-1:]]
        groups.insert(0, parts)
    matrix = transforms(groups, inflation[len(last) :])
    other = exchange(matrix, "row", 1)
    part = observed(last)
    own_parts, other_parts = [part], [exchange(part, "row", 1)]
    for bit in bits[-1:]:
        own_parts.append(exchange(part, "row", bit))
        other_parts.append(exchange(part, "row", bit | 1))
    first = close(own_parts, other_parts, anomaly_inflation[: 2 * len(last)], low_scalar)
    suffix, matrices = chain(first, matrix, other, low_scalar)
    whole = suffix[0]

    core_scalar = core.astype(jnp.int32).reshape(1)
    partner = exchange(whole, "tm", 1)
    coupled = couple(whole, partner, core_scalar)
    groups = lax.axis_size("tm") // 2
    later = []
    for ahead in range(1, groups):
        hop = 2 * ahead
        later.append(
            lax.ppermute(coupled, "tm", [(i + hop, i) for i in range(2 * groups - hop)])
        )
    filtered_ensemble = filtered(matrices, prior_ensemble)
    where = jnp.stack([place // 2, core]).astype(jnp.int32)
    smoothed_ensemble = smoothed(suffix, prior_ensemble, partner, later, where)
    return (smoothed_ensemble, filtered_ensemble)


def solution(mesh):
    placed = (
        P("tm", None, "row"),
        P("tm", "row"),
        P("row"),
        P("tm"),
        P("row", None, None, None),
        P("row", None),
    )
    return jax.shard_map(
        smoother,
        mesh=mesh,
        in_specs=placed,
        out_specs=(P("tm", None, "row"), P("tm", None, "row")),
        check_vma=False,
    )
```

```python
import functools

import jax
import jax.numpy as jnp
from jax import lax
from jax.experimental import pallas as pl
from jax.experimental.pallas import tpu as pltpu
from jax.sharding import PartitionSpec as P


NS_ITERS = 8
F32, BF16 = jnp.float32, jnp.bfloat16
exact_product = lax.Precision.HIGHEST
MEAN_ROWS = 16
PIECES = 4
SHARED = 1


def split(value):
    high = value.astype(BF16)
    return high, (value - high.astype(F32)).astype(BF16)


def product(left, right):
    return jnp.dot(left, right, precision=exact_product, preferred_element_type=F32)


def thirds(value):
    first = value.astype(BF16)
    rest = value - first.astype(F32)
    second = rest.astype(BF16)
    return first, second, (rest - second.astype(F32)).astype(BF16)


def stacked_product(left, right):
    size = right.shape[0]
    a, b, c = thirds(left)
    x, y, z = thirds(right)
    wide = jnp.concatenate([jnp.concatenate([x, y], axis=1)] * 2, axis=0)
    main = jnp.dot(jnp.concatenate([a, b], axis=1), wide, preferred_element_type=F32)
    rest = jnp.dot(
        jnp.concatenate([a, c], axis=1),
        jnp.concatenate([z, x], axis=0),
        preferred_element_type=F32,
    )
    return main[:, :size] + (main[:, size:] + rest)


def by_rows(left, right):
    return lax.dot_general(left, right, (((1,), (1,)), ((), ())), preferred_element_type=F32)


def eye(size):
    rows = lax.broadcasted_iota(jnp.int32, (size, size), 0)
    columns = lax.broadcasted_iota(jnp.int32, (size, size), 1)
    return (rows == columns).astype(F32)


def params(limit):
    return pltpu.CompilerParams(vmem_limit_bytes=limit << 20)


def prepare_body(sets, count, order_ref, spread_ref, *refs):
    out = refs[-1]
    size = spread_ref.shape[-1]
    for number in range(count):
        tiles = [refs[column * count + number] for column in range(sets)]
        each = tiles[0].shape[0]

        def emit(row, _):
            at = order_ref[number] * each + row
            scale = jnp.transpose(jnp.broadcast_to(spread_ref[at], (size, size)))
            start = 0
            for tile_ref in tiles:
                for k in range(tile_ref.shape[1]):
                    high, low = split(tile_ref[row, k] * scale)
                    out[at, :size, start : start + size] = high
                    out[at, size:, start : start + size] = low
                    start += size
            return 0

        lax.fori_loop(0, each, emit, 0)


def prepare(sets, order, spread):
    count, (each, k, size, _) = len(sets[0]), sets[0][0].shape
    flat = [piece for pieces in sets for piece in pieces]
    total = spread.shape[0]
    vmem = pl.BlockSpec(memory_space=pltpu.VMEM)
    return pl.pallas_call(
        functools.partial(prepare_body, len(sets), count),
        in_specs=[pl.BlockSpec(memory_space=pltpu.SMEM), vmem] + [vmem] * len(flat),
        out_specs=vmem,
        out_shape=pltpu.VMEM((total, 2 * size, len(sets) * k * size), BF16),
        compiler_params=params(10),
        cost_estimate=pl.CostEstimate(
            flops=0,
            transcendentals=0,
            bytes_accessed=len(flat) * each * k * size * size * 8,
        ),
        name="prepare",
    )(order, spread, *flat)


def observe_body(steps, shards, groups, places, target_ref, row_ref, data_ref, *refs):
    tiles = refs[: sum(groups)]
    states = refs[len(tiles) : len(tiles) + steps * shards]
    out, seen_ref, gram_ref = refs[len(tiles) + len(states) :]
    size = out.shape[-1]
    members = size
    rows = steps * members
    all_rows = rows + MEAN_ROWS
    blocks = states[0].shape[-1] // size
    slot_row = lax.broadcasted_iota(jnp.int32, (MEAN_ROWS, size), 0)
    for mask in range(shards):
        first = (row_ref[0] ^ mask) * blocks
        for block in range(blocks):
            columns = slice(block * size, (block + 1) * size)
            means = jnp.zeros((MEAN_ROWS, size), F32)
            for i in range(steps):
                value = states[i * shards + mask][places[i * shards + mask], :, columns]
                mean = jnp.mean(value, axis=0, keepdims=True)
                high, low = split(value - mean)
                at = i * members
                seen_ref[first + block, at : at + members] = high
                seen_ref[first + block, all_rows + at : all_rows + at + members] = low
                high, low = split(mean)
                means = jnp.where(slot_row == i, high.astype(F32), means)
                means = jnp.where(slot_row == MEAN_ROWS // 2 + i, low.astype(F32), means)
            seen_ref[first + block, rows:all_rows] = means.astype(BF16)
    gram_ref[...] = jnp.zeros_like(gram_ref)
    nonzero = target_ref.shape[1]

    def visit(base, parts, at_once, step, _):
        seen = []
        for j in range(at_once):
            at = step * at_once + j
            left = jnp.concatenate(
                [seen_ref[target_ref[base + at, k]] for k in range(nonzero)], axis=1
            )
            right = jnp.concatenate([part[at] for part in parts], axis=1)
            both = by_rows(left, right)
            both = both[:, :size] + both[:, size:]
            means = both[rows : rows + MEAN_ROWS // 2] + both[rows + MEAN_ROWS // 2 : all_rows]
            seen.append((both[:rows] + both[all_rows:], means))
        for j in range(0, at_once, 2):
            two = seen[j : j + 2]
            at = base + step * at_once + j
            for i in range(steps):
                white = jnp.concatenate(
                    [value[i * members : (i + 1) * members] for value, _ in two], axis=1
                )
                white_high, white_low = split(white)
                innovation = jnp.concatenate(
                    [
                        data_ref[i, at + n] - means[i : i + 1]
                        for n, (_, means) in enumerate(two)
                    ],
                    axis=1,
                )
                inn_high, inn_low = split(innovation)
                wide_row = lax.broadcasted_iota(jnp.int32, (MEAN_ROWS, len(two) * size), 0)
                extra = jnp.where(
                    wide_row == 0,
                    inn_high.astype(F32),
                    jnp.where(wide_row == 1, inn_low.astype(F32), 0.0),
                ).astype(BF16)
                gram_ref[i] += by_rows(
                    jnp.concatenate([white_high, extra], axis=0),
                    jnp.concatenate([white_high, white_low], axis=0),
                )
        return 0

    base, start = 0, 0
    for group in groups:
        parts = tiles[start : start + group]
        count = parts[0].shape[0]
        at_once = min(16 if steps == 1 else 8, count)
        lax.fori_loop(
            0, count // at_once, functools.partial(visit, base, parts, at_once), 0
        )
        base, start = base + count, start + group
    for i in range(steps):
        total = gram_ref[i]
        cross = total[:members, members:]
        out[i, :members] = total[:members, :members] + cross + jnp.transpose(cross)
        vector = (
            total[members : members + 1, :members]
            + total[members : members + 1, members:]
            + total[members + 1 : members + 2, :members]
        )
        out[i, members:] = jnp.broadcast_to(vector, (8, members))


def observe(chunk, states, tile_groups, targets, data, row):
    steps, shards = len(chunk), len(states[0])
    tiles = [part for group in tile_groups for part in group]
    _, double, _ = tiles[0].shape
    size = double // 2
    members = size
    columns = states[0][0][0].shape[-1]
    places = [g for pieces in states for _, g in pieces]
    flat = [piece for pieces in states for piece, _ in pieces]
    vmem = pl.BlockSpec(memory_space=pltpu.VMEM)
    smem = pl.BlockSpec(memory_space=pltpu.SMEM)
    in_specs = [smem, smem, vmem] + [vmem] * (len(tiles) + len(flat))
    slots = shards * (columns // size)
    rows = steps * members + MEAN_ROWS
    total, nonzero = targets.shape
    groups = [len(group) for group in tile_groups]
    return pl.pallas_call(
        functools.partial(observe_body, steps, shards, groups, places),
        in_specs=in_specs,
        out_specs=vmem,
        scratch_shapes=[
            pltpu.VMEM((slots, rows + steps * members, size), BF16),
            pltpu.VMEM((steps, members + MEAN_ROWS, 2 * members), F32),
        ],
        out_shape=jax.ShapeDtypeStruct((steps, members + 8, members), F32),
        compiler_params=params(18),
        cost_estimate=pl.CostEstimate(
            flops=2 * 4 * rows * size * nonzero * size * total,
            transcendentals=0,
            bytes_accessed=total * double * nonzero * size * 2,
        ),
        name="observe",
    )(targets, row, data, *tiles, *flat)


def roots(info_and_vectors, inflations, size):
    identity = eye(size)
    info = [value[:size] + identity for value in info_and_vectors]
    vector = [value[size:] for value in info_and_vectors]
    bound = [
        jnp.max(jnp.sum(jnp.abs(value), axis=1, keepdims=True), axis=0, keepdims=True)
        for value in info
    ]
    scaled = [value / top for value, top in zip(info, bound)]
    update = [1.5 * identity - 0.5 * value for value in scaled]
    inverse = update
    root = [stacked_product(value, up) for value, up in zip(scaled, update)]
    for number in range(1, NS_ITERS):
        update = [1.5 * identity - 0.5 * stacked_product(q, y) for q, y in zip(inverse, root)]
        if number < NS_ITERS - 1:
            both = [
                stacked_product(jnp.concatenate([y, q], axis=0), up)
                for y, q, up in zip(root, inverse, update)
            ]
            root = [value[:size] for value in both]
            inverse = [value[size:] for value in both]
        else:
            inverse = [stacked_product(q, up) for q, up in zip(inverse, update)]
    matrices = []
    for i, inflation in enumerate(inflations):
        half_root = inverse[i] / jnp.sqrt(bound[i])
        half = lax.dot_general(
            vector[i],
            half_root,
            (((1,), (1,)), ((), ())),
            precision=exact_product,
            preferred_element_type=F32,
        )
        weights = jnp.sum(half_root * half[:1], axis=1, keepdims=True)
        mixing = weights + inflation * half_root
        mixing = mixing - jnp.mean(mixing, axis=0, keepdims=True)
        matrices.append(mixing + 1.0 / size)
    return matrices


def transform_body(parts, inflation_ref, *refs):
    ins, out = refs[:-1], refs[-1]
    sums = []
    for start in range(0, len(ins), parts):
        group = ins[start : start + parts]
        for i in range(group[0].shape[0]):
            sums.append(sum((ref[i] for ref in group[1:]), group[0][i]))
    inflations = [inflation_ref[i] for i in range(len(sums))]
    for i, matrix in enumerate(roots(sums, inflations, out.shape[-1])):
        out[i] = matrix


def transforms(groups, inflation):
    parts = len(groups[0])
    flat = [part for group in groups for part in group]
    steps, members = sum(group[0].shape[0] for group in groups), flat[0].shape[-1]
    vmem = pl.BlockSpec(memory_space=pltpu.VMEM)
    return pl.pallas_call(
        functools.partial(transform_body, parts),
        in_specs=[pl.BlockSpec(memory_space=pltpu.SMEM)] + [vmem] * len(flat),
        out_specs=vmem,
        out_shape=jax.ShapeDtypeStruct((steps, members, members), F32),
        compiler_params=params(8),
        cost_estimate=pl.CostEstimate(
            flops=steps * 21 * 6 * 2 * members**3 * 4,
            transcendentals=0,
            bytes_accessed=steps * members * members * 12,
        ),
        name="transforms",
    )(inflation, *flat)


def chain_body(steps, low_ref, *refs):
    mine, other = refs[:2]
    later = refs[2:-3]
    whole_ref, suffix_ref, all_ref = refs[-3:]
    size = whole_ref.shape[-1]
    even = low_ref[0] == 0
    running = later[0][...] if later else None
    for i in reversed(range(steps)):
        for half, matrix in (
            (1, jnp.where(even, other[i], mine[i])),
            (0, jnp.where(even, mine[i], other[i])),
        ):
            at = (2 * i + half) * size
            all_ref[:, at : at + size] = jnp.transpose(matrix)
            running = matrix if running is None else stacked_product(matrix, running)
            suffix_ref[:, at : at + size] = jnp.transpose(running)
    whole_ref[...] = running


def chain(mine, other, later, low):
    steps, size, _ = mine.shape
    vmem = pl.BlockSpec(memory_space=pltpu.VMEM)
    args = [mine, other] + ([] if later is None else [later])
    return pl.pallas_call(
        functools.partial(chain_body, steps),
        in_specs=[pl.BlockSpec(memory_space=pltpu.SMEM)] + [vmem] * len(args),
        out_specs=(vmem, vmem, vmem),
        out_shape=(jax.ShapeDtypeStruct((size, size), F32),)
        + (jax.ShapeDtypeStruct((size, 2 * steps * size), F32),) * 2,
        compiler_params=params(6),
        cost_estimate=pl.CostEstimate(
            flops=2 * steps * 6 * 2 * size**3 * 8,
            transcendentals=0,
            bytes_accessed=steps * size * size * 32,
        ),
        name="chain",
    )(low, *args)


def couple_body(core_ref, mine, other, out):
    first = core_ref[0] == 0
    out[...] = stacked_product(
        jnp.where(first, mine[...], other[...]), jnp.where(first, other[...], mine[...])
    )


def couple(mine, other, core):
    vmem = pl.BlockSpec(memory_space=pltpu.VMEM)
    return pl.pallas_call(
        couple_body,
        in_specs=[pl.BlockSpec(memory_space=pltpu.SMEM), vmem, vmem],
        out_specs=vmem,
        out_shape=jax.ShapeDtypeStruct(mine.shape, F32),
        compiler_params=params(4),
        name="couple",
    )(core, mine, other)


def weigh_steps(weights_of, states_of, out_ref, buffer_ref, sems):
    steps = buffer_ref.shape[0]

    def copy(step):
        return pltpu.make_async_copy(buffer_ref.at[step], out_ref.at[step], sems.at[step])

    for step in range(steps):
        weights = weights_of(step)
        size = weights.shape[-1]
        state_high, state_low = states_of(step)
        both = jnp.dot(weights, state_high, preferred_element_type=F32)
        rest = jnp.dot(weights[:size], state_low, preferred_element_type=F32)
        buffer_ref[step] = both[:size] + both[size:] + rest
        copy(step).start()
    for step in range(steps):
        copy(step).wait()


def filtered_body(*refs):
    weights, (state_ref, out_ref, high_ref, low_ref, buffer_ref, sems) = refs[:-6], refs[-6:]
    size = state_ref.shape[1]
    matrices = [
        ref[:, at : at + size] for ref in weights for at in range(0, ref.shape[-1], size)
    ]

    def states_of(step):
        high, low = split(state_ref[step])
        high_ref[step] = high
        low_ref[step] = low
        return high, low

    weigh_steps(
        lambda step: jnp.concatenate(split(matrices[step]), axis=0),
        states_of,
        out_ref,
        buffer_ref,
        sems,
    )


def weighing(body, args, shape, smem_count, parts):
    steps, members, columns = shape
    vmem = pl.BlockSpec(memory_space=pltpu.VMEM)
    smem = pl.BlockSpec(memory_space=pltpu.SMEM)
    return pl.pallas_call(
        body,
        in_specs=[smem] * smem_count + [vmem] * (len(args) - smem_count),
        out_specs=(pl.BlockSpec(memory_space=pl.ANY),) + (vmem,) * parts,
        out_shape=(jax.ShapeDtypeStruct(shape, F32),) + (pltpu.VMEM(shape, BF16),) * parts,
        scratch_shapes=[
            pltpu.VMEM(shape, F32),
            pltpu.SemaphoreType.DMA((steps,)),
        ],
        compiler_params=params(14),
        cost_estimate=pl.CostEstimate(
            flops=steps * 3 * 2 * members * members * columns,
            transcendentals=0,
            bytes_accessed=steps * members * columns * 8,
        ),
    )(*args)


def smooth_body(groups, place_ref, *refs):
    partner_ref, later, suffixes = refs[0], refs[1:groups], refs[groups:-5]
    high_ref, low_ref, out_ref, buffer_ref, sems = refs[-5:]
    size = partner_ref.shape[-1]
    identity = eye(size)
    chain = [jnp.where(place_ref[1] == 0, partner_ref[...], identity)]
    for group in range(1, groups):
        value = identity
        for mask, ref in enumerate(later, 1):
            value = jnp.where(place_ref[0] ^ mask == group, ref[...], value)
        chain.append(jnp.where(place_ref[0] < group, value, identity))
    while len(chain) > 1:
        joined = [stacked_product(a, b) for a, b in zip(chain[::2], chain[1::2])]
        chain = joined + ([chain[-1]] if len(chain) % 2 else [])
    end = jnp.transpose(chain[0])
    totals = []
    for ref in suffixes:
        total = product(end, ref[...])
        totals += [total[:, at : at + size] for at in range(0, total.shape[-1], size)]
    weigh_steps(
        lambda step: jnp.concatenate(split(totals[step]), axis=0),
        lambda step: (high_ref[step], low_ref[step]),
        out_ref,
        buffer_ref,
        sems,
    )


def exchange(value, axis, bit):
    count = lax.axis_size(axis)
    return lax.ppermute(value, axis, [(i, i ^ bit) for i in range(count)])


def smoother(
    prior_ensemble,
    observation_data,
    inverse_error_spread,
    anomaly_inflation,
    nonzero_tiles,
    nonzero_tile_targets,
):
    steps, members, columns = prior_ensemble.shape
    block_rows, nonzero, size, _ = nonzero_tiles.shape
    shards = lax.axis_size("row")
    row, place = lax.axis_index("row"), lax.axis_index("tm")
    low, core = row & 1, place & 1
    pairs = steps // 2
    early, last = ((2, 3), (1,)), (0,)
    chunks = early + (last,)
    sequence = [g for chunk in chunks for g in reversed(chunk)]
    bits = []
    while 2 << len(bits) < shards:
        bits.append(2 << len(bits))

    spread = inverse_error_spread / float(members - 1) ** 0.5
    data = observation_data * spread
    halves = data.reshape(pairs, 2, -1)
    of_low = functools.partial(lax.dynamic_index_in_dim, axis=1, keepdims=False)
    padded = jnp.zeros((data.shape[1],), F32)
    padded = padded.at[: nonzero_tile_targets.size].set(nonzero_tile_targets.reshape(-1).astype(F32))
    note = jnp.concatenate([of_low(halves, 1 - low), spread[None], padded[None]], axis=0)
    quarter = place & 3
    each = block_rows // 4
    cut = nonzero // PIECES
    half, far = cut // 2, (place >> 2) & 1
    fetched, source = [], nonzero_tiles
    for part in range(PIECES):
        shared = part < SHARED
        start = part * cut + (far * half if shared else 0)
        group = lax.dynamic_slice(
            source, (quarter * each, start, 0, 0), (each, half if shared else cut, size, size)
        )
        if part == 0:
            group, source = lax.optimization_barrier((group, source))
        group = exchange(group, "row", 1)
        if shared:
            distant = exchange(group, "tm", 4)
            group = jnp.concatenate(
                [jnp.where(far == 0, group, distant), jnp.where(far == 0, distant, group)],
                axis=1,
            )
        fetched.append(group)
    note = exchange(note, "row", 1)
    states = prior_ensemble.reshape(pairs, 2, members, columns)
    mine, theirs = of_low(states, low), of_low(states, 1 - low)
    sent = {g: exchange(theirs[g : g + 1], "row", 1) for g in sequence}
    around = {g: exchange(theirs[g : g + 1], "row", 2) for g in sequence[-1:]}
    forward = {g: exchange(around[g], "row", 1) for g in sequence[-1:]}
    mine = {g: mine[g : g + 1] for g in sequence}
    pieces = {}
    for g in sequence:
        have = [(mine[g], 0), (sent[g], 0)]
        for bit in bits:
            moved = [(exchange(mine[g], "row", bit), 0)]
            for value, at in have[1:]:
                if g in forward and bit == 2:
                    moved.append((forward[g], 0))
                else:
                    moved.append((exchange(value[at : at + 1], "row", bit), 0))
            have = have + moved
        pieces[g] = have

    per_row = spread.reshape(block_rows, 1, size)
    own_tiles = prepare([[nonzero_tiles]], jnp.zeros((1,), jnp.int32), per_row)
    their_data = note[:pairs].reshape(pairs, block_rows, 1, size)
    own_data = of_low(halves, low).reshape(pairs, block_rows, 1, size)
    all_data = jnp.concatenate([own_data, their_data], axis=1)
    their_spread = note[pairs].reshape(block_rows, 1, size)
    their_targets = note[pairs + 1, : nonzero_tile_targets.size].astype(jnp.int32)
    targets = jnp.concatenate(
        [nonzero_tile_targets, their_targets.reshape(block_rows, nonzero)], axis=0
    )
    order = jnp.stack([quarter, quarter ^ 2, quarter ^ 1, quarter ^ 3]).astype(jnp.int32)
    their_tiles, arrived = [], []
    for part, value in enumerate(fetched):
        across = exchange(value, "tm", 2)
        beside = exchange(value, "tm", 1)
        arrived.append([value, across, beside, exchange(across, "tm", 1)])
    for part in range(0, PIECES, 2):
        their_tiles.append(prepare(arrived[part : part + 2], order, their_spread))
    tile_groups = [[own_tiles], their_tiles]

    row_scalar = row.astype(jnp.int32).reshape(1)
    low_scalar = low.astype(jnp.int32).reshape(1)
    inflation = of_low(anomaly_inflation.reshape(pairs, 2), low)

    def observed(chunk):
        part = observe(
            chunk,
            [pieces[g] for g in chunk],
            tile_groups,
            targets,
            all_data[chunk[0] : chunk[0] + len(chunk)],
            row_scalar,
        )
        for bit in bits[:-1]:
            part = part + exchange(part, "row", bit)
        return part

    groups = []
    for chunk in early:
        part = observed(chunk)
        parts = [part] + [exchange(part, "row", bit) for bit in bits[-1:]]
        groups.insert(0, parts)
    matrix = transforms(groups, inflation[len(last) :])
    other = exchange(matrix, "row", 1)
    part = observed(last)
    parts = [part] + [exchange(part, "row", bit) for bit in bits[-1:]]
    first = transforms([parts], inflation[: len(last)])
    first_other = exchange(first, "row", 1)
    later_whole, later_suffix, later_all = chain(matrix, other, None, low_scalar)
    whole, first_suffix, first_all = chain(first, first_other, later_whole, low_scalar)

    core_scalar = core.astype(jnp.int32).reshape(1)
    partner = exchange(whole, "tm", 1)
    coupled = couple(whole, partner, core_scalar)
    groups = lax.axis_size("tm") // 2
    later = [exchange(coupled, "tm", 2 * mask) for mask in range(1, groups)]
    filtered_ensemble, high, rest = weighing(
        filtered_body, [first_all, later_all, prior_ensemble], prior_ensemble.shape, 0, 2
    )
    where = jnp.stack([place // 2, core]).astype(jnp.int32)
    (smoothed_ensemble,) = weighing(
        functools.partial(smooth_body, groups),
        [where, partner, *later, first_suffix, later_suffix, high, rest],
        prior_ensemble.shape,
        1,
        0,
    )
    return (smoothed_ensemble, filtered_ensemble)


def solution(mesh):
    placed = (
        P("tm", None, "row"),
        P("tm", "row"),
        P("row"),
        P("tm"),
        P("row", None, None, None),
        P("row", None),
    )
    return jax.shard_map(
        smoother,
        mesh=mesh,
        in_specs=placed,
        out_specs=(P("tm", None, "row"), P("tm", None, "row")),
        check_vma=False,
    )
```
